32 devices in a mesh: dp: 8 (over z, y), tensor: 4 (over x, core).
Axes of the slice: x: 2, y: 2, z: 4, core: 2. Of those that a mesh axis runs over, the one named last changes fastest.
Arguments:
- activations: bfloat16 [2048, 8192], P('dp'), may hold values from -6 to 6
- key_value_grads: bfloat16 [2048, 2, 1024], P('dp', None, 'tensor'), may hold values from -6 to 6
- owner_table: int32 [64], replicated, may hold values from 0 to 63, each once
- left_factors: float32 [4, 64, 512, 512], P('tensor', 'dp'), may hold values from -16 to 16, as said below
- right_factors: float32 [4, 64, 128, 128], P('tensor', 'dp'), may hold values from -16 to 16, as said below
Outputs:
- left_updated: float32 [4, 64, 512, 512], P('tensor', 'dp')
- right_updated: float32 [4, 64, 128, 128], P('tensor', 'dp')
- update: bfloat16 [2, 8192, 1024], P(None, 'dp')
The draws below stay inside these ranges and needn't reach their ends.
Inputs may be any that keep to these rules, and one draw needn't show every extreme that they name: `owner_table`: each block number appears once; slot s lies on index s // 8 of dp. `left_factors`: every block is symmetric positive definite. `right_factors`: every block is symmetric positive definite.
All inputs are finite; a program needn't handle non-finite values.
Results may differ from the reference program's by a relative error of at most 0.012.
The reference program's roundings to bfloat16 on the way (of `direction`) count: a program that leaves them out, or rounds other values in their place, can miss the bound.
Values may be sent and summed in bfloat16 or wider, within the bound.
A program may use at most 128 MiB of HBM per device.

```python
import jax
import jax.numpy as jnp
from jax import lax

D = 8192
KVW = 1024
BC = 128
BL = 512
ITERS = 8
TOKENS = 2048
TSH = 4
CB = 2
NRB = 16
NBLK = 64


def factor_draw(base_key, salt_value, order_dim, scale_value):
    mixed_key = jax.random.fold_in(base_key, salt_value)
    first_key = jax.random.fold_in(mixed_key, 0)
    base_draw = jax.random.normal(first_key, (TSH, NBLK, order_dim, order_dim), jnp.float32)
    wishart = jnp.einsum('tsik,tsjk->tsij', base_draw, base_draw) / order_dim
    shaped = wishart + 0.25 * jnp.eye(order_dim, dtype=jnp.float32)
    return shaped * scale_value


def draw_left_factors(key, part):
    return factor_draw(key, 11, BL, BC / TOKENS)


def draw_right_factors(key, part):
    return factor_draw(key, 23, BC, BL / TOKENS)


def with_spikes(values, rng, source, target, shards_of, factor):
    def block_of(position):
        return (jnp.arange(values.shape[position]) // (values.shape[position] // shards_of)).reshape((-1,) + (1,) * (values.ndim - 1 - position))

    first = jax.random.permutation(rng, shards_of)[block_of(target)]
    far = (block_of(target) + shards_of // 2) % shards_of
    return jnp.where((block_of(source) == first) | (block_of(source) == far), factor * values, values)


def block_scale(key, dims, shards, low, high):
    def one(position, shards_of):
        steps = jax.random.uniform(jax.random.fold_in(jax.random.fold_in(key, 6), position), (shards_of,), jnp.float32, low / len(shards), high / len(shards))
        return jnp.repeat(jnp.exp(steps), dims[position] // shards_of).reshape((-1,) + (1,) * (len(dims) - position - 1))

    gain = one(*shards[0])
    for cut in shards[1:]:
        gain = gain * one(*cut)
    return gain


def centred(key, extent, width, limit, pieces=(), kind=jnp.bfloat16):
    entries = jax.random.normal(key, extent, jnp.float32) * width
    if len(pieces) > 0:
        entries = block_scale(key, extent, pieces, -0.22, 0.18) * entries
    return jnp.clip(entries, min=-limit, max=limit).astype(kind)


def heavy_noise(rng, dims, scale, reach, cuts, heavy, held_as=jnp.bfloat16):
    values = scale * jax.random.normal(rng, dims, jnp.float32)
    if cuts:
        values = values * block_scale(rng, dims, cuts, -0.22, 0.18)
    return jnp.clip(with_spikes(values, jax.random.fold_in(rng, 3), *heavy), -reach, reach).astype(held_as)


def setup_inputs(seed: int = 0) -> dict:
    arg_keys = jax.random.split(jax.random.key(seed), 6)
    activations = heavy_noise(arg_keys[0], (TOKENS, D), 1.0, 6.0, ((0, 8),), (0, 1, 8, 2.0))
    key_value_grads = centred(arg_keys[1], (TOKENS, 2, KVW), 1.0, 6.0, ((0, 8), (2, 4)))
    owner_table = jax.random.permutation(arg_keys[2], NBLK).astype(jnp.int32)
    left_factors = draw_left_factors(jax.random.fold_in(arg_keys[5], 71), 0)
    right_factors = draw_right_factors(jax.random.fold_in(arg_keys[5], 71), 0)
    return dict(activations=activations, key_value_grads=key_value_grads, owner_table=owner_table, left_factors=left_factors, right_factors=right_factors)


MOMENT_DECAY = 0.9
RIDGE_SHARE = 0.0001
EXACT_MODE = lax.Precision.HIGHEST

def product(left_mat, right_mat):
    return jnp.dot(left_mat, right_mat, precision=EXACT_MODE, preferred_element_type=jnp.float32)

def rounded(matrix):
    narrow = lax.optimization_barrier(matrix.astype(jnp.bfloat16))
    return narrow.astype(jnp.float32)

def coarse_product(left_mat, right_mat):
    return product(rounded(left_mat), rounded(right_mat))

def inverse_root(matrix):
    order_dim = matrix.shape[0]
    identity_mat = jnp.eye(order_dim, dtype=jnp.float32)
    shifted = matrix + RIDGE_SHARE * jnp.trace(matrix) / order_dim * identity_mat
    scaling = 2.5 / jnp.sqrt(jnp.sum(shifted * shifted))
    result = jnp.sqrt(jnp.sqrt(scaling)) * identity_mat
    powered = scaling * shifted
    for iteration in range(ITERS):
        factor = (5.0 * identity_mat - powered) * 0.25
        result = coarse_product(result, factor)
        if iteration + 1 < ITERS:
            squared = coarse_product(factor, factor)
            powered = coarse_product(coarse_product(squared, squared), powered)
    return result

def block_step(inputs):
    gradient, left_old, right_old = inputs
    left_new = MOMENT_DECAY * left_old + (1.0 - MOMENT_DECAY) * product(gradient, gradient.T)
    right_new = MOMENT_DECAY * right_old + (1.0 - MOMENT_DECAY) * product(gradient.T, gradient)
    precond = product(product(inverse_root(left_new), gradient), inverse_root(right_new))
    direction = precond / jnp.sqrt(jnp.mean(precond * precond) + 1e-06)
    return (left_new, right_new, direction.astype(jnp.bfloat16))

def reference(activations, key_value_grads, owner_table, left_factors, right_factors):
    sums = []
    for which in range(2):
        sums.append(jnp.dot(activations.T, key_value_grads[:, which, :], preferred_element_type=jnp.float32) / TOKENS)
    full_grad = jnp.stack(sums)
    canonical = full_grad.reshape(2, NRB, BL, TSH, CB, BC).transpose(3, 0, 1, 4, 2, 5).reshape(TSH, NBLK, BL, BC)
    by_slot = jnp.take(canonical, owner_table, axis=1)
    left_new, right_new, directions = lax.map(block_step, (by_slot.reshape(TSH * NBLK, BL, BC), left_factors.reshape(TSH * NBLK, BL, BL), right_factors.reshape(TSH * NBLK, BC, BC)))
    directions = directions.reshape(TSH, NBLK, BL, BC)
    placed = jnp.zeros((TSH, NBLK, BL, BC), jnp.bfloat16).at[:, owner_table].set(directions)
    update = placed.reshape(TSH, 2, NRB, CB, BL, BC).transpose(1, 2, 4, 0, 3, 5).reshape(2, D, KVW)
    return (left_new.reshape(TSH, NBLK, BL, BL), right_new.reshape(TSH, NBLK, BC, BC), update)
```

```python
import functools

import jax
import jax.numpy as jnp
from jax import lax
from jax.experimental import pallas as pl
from jax.experimental.pallas import tpu as pltpu
from jax.sharding import PartitionSpec as P

ITERS = 8
MOMENT_DECAY = 0.9
RIDGE_SHARE = 0.0001
CHUNK_SLOTS = 2
VMEM_LIMIT = 60 * 1024 * 1024


def dot(left_mat, right_mat):
    return jnp.dot(left_mat, right_mat, preferred_element_type=jnp.float32)


def halves(x):
    high = x.astype(jnp.bfloat16)
    low = (x - high.astype(jnp.float32)).astype(jnp.bfloat16)
    return high, low


def gradient_kernel(
    table_ref, act_ref, kv_ref, out_ref, *, chunk, chunk_slots, slots, per_projection, col_blocks, scale
):
    rows_block, cols_block = out_ref.shape[2:]
    width = col_blocks * cols_block
    first = pl.program_id(0) * slots + chunk * chunk_slots
    for k in range(chunk_slots):
        block_id = table_ref[first + k]
        projection = block_id // per_projection
        remainder = block_id % per_projection
        row_start = pl.multiple_of(remainder // col_blocks * rows_block, rows_block)
        col_start = pl.multiple_of(
            projection * width + remainder % col_blocks * cols_block, cols_block
        )
        summed = lax.dot_general(
            act_ref[:, pl.ds(row_start, rows_block)],
            kv_ref[:, pl.ds(col_start, cols_block)],
            (((0,), (0,)), ((), ())),
            preferred_element_type=jnp.float32,
        )
        out_ref[0, k] = summed * scale


def gradient_chunk(table, activations, cotangents, chunk, chunk_slots, ranks, rows_block, cols_block, col_blocks):
    tokens, model = activations.shape
    slots = table.shape[0] // ranks
    body = functools.partial(
        gradient_kernel,
        chunk=chunk,
        chunk_slots=chunk_slots,
        slots=slots,
        per_projection=model // rows_block * col_blocks,
        col_blocks=col_blocks,
        scale=1.0 / (tokens * ranks),
    )
    return pl.pallas_call(
        body,
        out_shape=jax.ShapeDtypeStruct((ranks, chunk_slots, rows_block, cols_block), jnp.float32),
        grid_spec=pltpu.PrefetchScalarGridSpec(
            num_scalar_prefetch=1,
            grid=(ranks,),
            in_specs=[
                pl.BlockSpec(activations.shape, lambda d, t: (0, 0), pipeline_mode=pl.Buffered(1)),
                pl.BlockSpec(cotangents.shape, lambda d, t: (0, 0), pipeline_mode=pl.Buffered(1)),
            ],
            out_specs=pl.BlockSpec(
                (1, chunk_slots, rows_block, cols_block), lambda d, t: (d, 0, 0, 0)
            ),
        ),
        compiler_params=pltpu.CompilerParams(vmem_limit_bytes=VMEM_LIMIT),
        cost_estimate=pl.CostEstimate(
            flops=2 * ranks * chunk_slots * rows_block * cols_block * tokens,
            bytes_accessed=activations.size * 2 + ranks * chunk_slots * rows_block * cols_block * 4,
            transcendentals=0,
        ),
    )(table, activations, cotangents)


def diagonal(order):
    rows = lax.broadcasted_iota(jnp.int32, (order, order), 0)
    return rows == lax.broadcasted_iota(jnp.int32, (order, order), 1)


def total(x):
    return jnp.sum(jnp.sum(x, axis=1, keepdims=True), axis=0, keepdims=True)


def factor_of(powered, on_diagonal):
    return ((jnp.where(on_diagonal, 5.0, 0.0) - powered) * 0.25).astype(jnp.bfloat16)


def begin_root(updated, m_ref, f_ref, x_ref):
    order = updated.shape[0]
    on_diagonal = diagonal(order)
    trace = total(jnp.where(on_diagonal, updated, 0.0))
    shifted = updated + jnp.where(on_diagonal, RIDGE_SHARE * trace / order, 0.0)
    scaling = 2.5 / jnp.sqrt(total(shifted * shifted))
    powered = scaling * shifted
    factor = factor_of(powered, on_diagonal)
    start = jnp.sqrt(jnp.sqrt(scaling)).astype(jnp.bfloat16).astype(jnp.float32)
    m_ref[...] = powered.astype(jnp.bfloat16)
    f_ref[...] = factor
    x_ref[...] = start * factor.astype(jnp.float32)


def root_steps(groups):
    squares = []
    for m_ref, f_ref, x_ref in groups:
        factor = f_ref[...]
        squares.append(dot(factor, factor).astype(jnp.bfloat16))
    fourths = [dot(s, s).astype(jnp.bfloat16) for s in squares]
    for fourth, (m_ref, f_ref, x_ref) in zip(fourths, groups):
        powered = dot(fourth, m_ref[...])
        m_ref[...] = powered.astype(jnp.bfloat16)
        f_ref[...] = factor_of(powered, diagonal(powered.shape[0]))
    for m_ref, f_ref, x_ref in groups:
        x_ref[...] = dot(x_ref[...].astype(jnp.bfloat16), f_ref[...])


def block_kernel(grad_ref, left_ref, right_ref, *rest, chunk_slots, chained):
    if chained:
        rest = rest[2:]
    left_out, right_out, dir_ref, ml, fl, xl, mr, fr, xr = rest
    groups = []
    for k in range(chunk_slots):
        grad = grad_ref[k]
        high, low = halves(grad)
        flipped = grad.T
        high_t, low_t = halves(flipped)
        wide = jnp.concatenate([high, high, low], axis=1)
        wide_t = jnp.concatenate([high_t, high_t, low_t], axis=1)
        tall = jnp.concatenate([high, low, high], axis=0)
        tall_t = jnp.concatenate([high_t, low_t, high_t], axis=0)
        left_new = MOMENT_DECAY * left_ref[k] + (1.0 - MOMENT_DECAY) * dot(wide, tall_t)
        right_new = MOMENT_DECAY * right_ref[k] + (1.0 - MOMENT_DECAY) * dot(wide_t, tall)
        left_out[k] = left_new
        right_out[k] = right_new
        begin_root(left_new, ml.at[k], fl.at[k], xl.at[k])
        begin_root(right_new, mr.at[k], fr.at[k], xr.at[k])
        groups.append((ml.at[k], fl.at[k], xl.at[k]))
        groups.append((mr.at[k], fr.at[k], xr.at[k]))

    def step(_, carry):
        root_steps(groups)
        return carry

    lax.fori_loop(0, ITERS - 1, step, 0)
    for k in range(chunk_slots):
        high, low = halves(grad_ref[k])
        tall = jnp.concatenate([high, low, high], axis=0)
        root_high, root_low = halves(xl[k])
        half = dot(jnp.concatenate([root_high, root_high, root_low], axis=1), tall)
        half_high, half_low = halves(half)
        right_high, right_low = halves(xr[k])
        precond = dot(
            jnp.concatenate([half_high, half_high, half_low], axis=1),
            jnp.concatenate([right_high, right_low, right_high], axis=0),
        )
        mean = total(precond * precond) / precond.size
        dir_ref[k] = (precond / jnp.sqrt(mean + 1e-06)).astype(jnp.bfloat16)


def block_chunk(grads, left_factors, right_factors, chunk, before):
    chunk_slots, rows_block, cols_block = grads.shape

    def pick(*tail):
        return pl.BlockSpec((chunk_slots,) + tail, lambda g: (chunk, 0, 0))

    def whole(*tail):
        return pl.BlockSpec((chunk_slots,) + tail, lambda g: (0, 0, 0))

    chained = before is not None
    specs = [
        whole(rows_block, cols_block),
        pick(rows_block, rows_block),
        pick(cols_block, cols_block),
    ]
    operands = [grads, left_factors, right_factors]
    aliases = {}
    if chained:
        specs += [pl.BlockSpec(memory_space=pl.ANY)] * 2
        operands += list(before)
        aliases = {3: 0, 4: 1}

    def scratch(order):
        square = (chunk_slots, order, order)
        return [
            pltpu.VMEM(square, jnp.bfloat16),
            pltpu.VMEM(square, jnp.bfloat16),
            pltpu.VMEM(square, jnp.float32),
        ]

    return pl.pallas_call(
        functools.partial(block_kernel, chunk_slots=chunk_slots, chained=chained),
        grid=(1,),
        out_shape=(
            jax.ShapeDtypeStruct(left_factors.shape, jnp.float32),
            jax.ShapeDtypeStruct(right_factors.shape, jnp.float32),
            jax.ShapeDtypeStruct(grads.shape, jnp.bfloat16),
        ),
        in_specs=specs,
        out_specs=(
            pick(rows_block, rows_block),
            pick(cols_block, cols_block),
            whole(rows_block, cols_block),
        ),
        scratch_shapes=scratch(rows_block) + scratch(cols_block),
        input_output_aliases=aliases,
        compiler_params=pltpu.CompilerParams(vmem_limit_bytes=VMEM_LIMIT),
        cost_estimate=pl.CostEstimate(
            flops=2 * chunk_slots * rows_block**3 * 4 * ITERS,
            bytes_accessed=chunk_slots * rows_block * rows_block * 8,
            transcendentals=0,
        ),
    )(*operands)


def pick_kernel(dev_ref, pos_ref, sub_ref, *refs, shape, chunk_slots, piece_rows, cols_block):
    sources, out_ref, sem = refs[:-2], refs[-2], refs[-1]
    projections, per_shard, col_blocks = shape
    index = 0
    for projection in range(projections):
        for piece in range(per_shard):
            for column in range(col_blocks):
                dest = out_ref.at[
                    projection,
                    pl.ds(piece * piece_rows, piece_rows),
                    pl.ds(column * cols_block, cols_block),
                ]
                rows = pl.ds(pl.multiple_of(sub_ref[piece] * piece_rows, piece_rows), piece_rows)
                for chunk, source in enumerate(sources):

                    @pl.when(pos_ref[index] // chunk_slots == chunk)
                    def _():
                        pltpu.make_async_copy(
                            source.at[dev_ref[index], pos_ref[index] % chunk_slots, rows], dest, sem.at[index]
                        ).start()

                index += 1
    index = 0
    for projection in range(projections):
        for piece in range(per_shard):
            for column in range(col_blocks):
                dest = out_ref.at[
                    projection,
                    pl.ds(piece * piece_rows, piece_rows),
                    pl.ds(column * cols_block, cols_block),
                ]
                pltpu.make_async_copy(
                    sources[0].at[0, 0, pl.ds(0, piece_rows)], dest, sem.at[index]
                ).wait()
                index += 1


def pick_rows(gathered, owner_table, shard_rows, row_blocks, col_blocks, slots):
    _, chunk_slots, block_order, cols_block = gathered[0].shape
    piece_rows = min(shard_rows, block_order)
    per_block = block_order // piece_rows
    per_shard = shard_rows // piece_rows
    pieces = lax.axis_index("dp") * per_shard + jnp.arange(per_shard, dtype=jnp.int32)
    wanted = (
        jnp.arange(2, dtype=jnp.int32)[:, None, None] * row_blocks + (pieces // per_block)[None, :, None]
    ) * col_blocks + jnp.arange(col_blocks, dtype=jnp.int32)[None, None, :]
    hits = wanted.reshape(-1)[:, None] == owner_table[None, :]
    where = jnp.sum(
        jnp.where(hits, jnp.arange(owner_table.shape[0], dtype=jnp.int32)[None, :], 0), axis=1, dtype=jnp.int32
    )
    count = 2 * per_shard * col_blocks
    body = functools.partial(
        pick_kernel,
        shape=(2, per_shard, col_blocks),
        chunk_slots=chunk_slots,
        piece_rows=piece_rows,
        cols_block=cols_block,
    )
    shape = (2, shard_rows, col_blocks * cols_block)
    return pl.pallas_call(
        body,
        out_shape=jax.ShapeDtypeStruct(shape, jnp.bfloat16),
        grid_spec=pltpu.PrefetchScalarGridSpec(
            num_scalar_prefetch=3,
            grid=(1,),
            in_specs=[pl.BlockSpec(memory_space=pl.ANY)] * len(gathered),
            out_specs=pl.BlockSpec(shape, lambda g, *_: (0, 0, 0)),
            scratch_shapes=[pltpu.SemaphoreType.DMA((count,))],
        ),
    )(where // slots, where % slots, pieces % per_block, *gathered)


def local(activations, key_value_grads, owner_table, left_factors, right_factors):
    rows_block = left_factors.shape[2]
    cols_block = right_factors.shape[2]
    ranks = lax.axis_size("dp")
    row_blocks = activations.shape[1] // rows_block
    col_blocks = key_value_grads.shape[2] // cols_block
    shard_rows = activations.shape[1] // ranks
    slots = left_factors.shape[1]
    chunk_slots = min(CHUNK_SLOTS, slots)
    cotangents = key_value_grads.reshape(key_value_grads.shape[0], -1)
    grads = []
    for chunk in range(slots // chunk_slots):
        partial = gradient_chunk(
            owner_table, activations, cotangents, chunk, chunk_slots, ranks, rows_block, cols_block, col_blocks
        )
        grads.append(lax.psum_scatter(partial, "dp", scatter_dimension=0, tiled=True)[0])
    before = None
    gathered = []
    for chunk, grad in enumerate(grads):
        left_new, right_new, directions = block_chunk(grad, left_factors[0], right_factors[0], chunk, before)
        before = (left_new, right_new)
        gathered.append(lax.all_gather(directions, "dp", axis=0))
    own_rows = pick_rows(gathered, owner_table, shard_rows, row_blocks, col_blocks, slots)
    update = lax.all_gather(own_rows, "tensor", axis=2, tiled=True)
    return (left_new[None], right_new[None], update)


def solution(mesh):
    in_specs = (
        P("dp", None),
        P("dp", None, "tensor"),
        P(),
        P("tensor", "dp", None, None),
        P("tensor", "dp", None, None),
    )
    out_specs = (P("tensor", "dp", None, None), P("tensor", "dp", None, None), P(None, "dp", None))
    return jax.shard_map(local, mesh=mesh, in_specs=in_specs, out_specs=out_specs, check_vma=False)
```
